32 devices in a mesh: seq: 16 (over z, y, x), mp: 2 (over core).
Axes of the slice: x: 2, y: 2, z: 4, core: 2. Of those that a mesh axis runs over, the one named last changes fastest.
Arguments:
- inner_act: bfloat16 [2048, 6144], P('seq', 'mp'), may hold values from -6 to 6
- gate_act: bfloat16 [2048, 6144], P('seq', 'mp'), may hold values from -6 to 6
- x_proj: bfloat16 [6144, 224], P('mp'), may hold values from -0.078125 to 0.078125
- dt_proj: bfloat16 [192, 6144], P(None, 'mp'), may hold values from -0.4375 to 0.4375
- dt_bias: float32 [6144], P('mp'), may hold values from -5.5 to -3.5
- a_log: float32 [16, 6144], P(None, 'mp'), may hold values from -12 to 2.3
- skip: float32 [6144], P('mp'), may hold values from 0.5 to 1.5
Outputs:
- mixed_out: bfloat16 [2048, 6144], P('seq', 'mp')
The draws below stay inside these ranges and needn't reach their ends.
All inputs are finite; a program needn't handle non-finite values.
Results may differ from the reference program's by a relative error of at most 0.0095.
Values sent between devices are 32-bit elements; how exact they have to be, the bound alone decides.
A program may use at most 128 MiB of HBM per device.

```python
import jax
import jax.numpy as jnp
from jax import lax

INNER = 6144
STATES = 16
DT_RANK = 192
TOKENS = 2048


def level_of(key, dims, pieces, least, largest):
    loudness, own = 1.0, jax.random.fold_in(key, 6)
    for dim, shards_of in pieces:
        heights = jnp.exp(jax.random.uniform(jax.random.fold_in(own, dim), (shards_of,), jnp.float32, least / len(pieces), largest / len(pieces)))
        loudness = loudness * jnp.repeat(heights, dims[dim] // shards_of).reshape([-1 if axis == dim else 1 for axis in range(len(dims))])
    return loudness


def gaussian(key, dims, scale, limit, cuts=(), dtype=jnp.bfloat16):
    level = level_of(key, dims, cuts, -0.22, 0.18) if cuts else 1.0
    entries = jax.random.normal(key, dims, jnp.float32) * scale * level
    return jnp.minimum(jnp.maximum(entries, -limit), limit).astype(dtype)


def setup_inputs(seed: int = 0) -> dict:
    keys = jax.random.split(jax.random.key(seed), 8)
    return {
        "inner_act": gaussian(keys[0], (TOKENS, INNER), 1.0, 6.0, ((0, 16), (1, 2))),
        "gate_act": gaussian(keys[1], (TOKENS, INNER), 1.0, 6.0, ((0, 16), (1, 2))),
        "x_proj": gaussian(keys[2], (INNER, DT_RANK + 2 * STATES), INNER ** -0.5, 0.078125, ((0, 2),)),
        "dt_proj": gaussian(keys[3], (DT_RANK, INNER), DT_RANK ** -0.5, 0.4375, ((1, 2),)),
        "dt_bias": jnp.clip(-5.5 + 2.0 * jax.random.uniform(keys[4], (INNER,), jnp.float32) ** level_of(keys[4], (INNER,), ((0, 2),), -0.2, 0.2), -5.5, -3.5),
        "a_log": jnp.clip(-12.0 + 14.3 * jax.random.uniform(keys[5], (STATES, INNER), jnp.float32) ** level_of(keys[5], (STATES, INNER), ((1, 2),), -0.2, 0.2), -12.0, 2.3),
        "skip": jnp.clip(0.5 + 1.0 * jax.random.uniform(keys[6], (INNER,), jnp.float32) ** level_of(keys[6], (INNER,), ((0, 2),), -0.2, 0.2), 0.5, 1.5),
    }


def recurrence(dt, drive, bmat, cmat, rate, init):
    total = dt.shape[0]
    count = total // 32

    def advance(state, block):
        dt_blk, drive_blk, b_blk, c_blk = block
        outputs = []
        for i in range(32):
            state = jnp.exp(-rate * dt_blk[i][None, :]) * state + b_blk[i][:, None] * drive_blk[i][None, :]
            outputs.append(jnp.sum(c_blk[i][:, None] * state, axis=0))
        return state, jnp.stack(outputs)

    blocks = (dt.reshape(count, 32, -1), drive.reshape(count, 32, -1),
              bmat.reshape(count, 32, -1), cmat.reshape(count, 32, -1))
    final, values = lax.scan(advance, init, blocks)
    return values.reshape(total, -1), final


def reference(inner_act, gate_act, x_proj, dt_proj, dt_bias, a_log, skip):
    proj = jnp.dot(inner_act, x_proj, preferred_element_type=jnp.float32)
    rank = dt_proj.shape[0]
    states = a_log.shape[0]
    low = proj[:, :rank].astype(jnp.bfloat16)
    dt = jax.nn.softplus(jnp.dot(low, dt_proj, preferred_element_type=jnp.float32) + dt_bias[None, :])
    bmat = proj[:, rank:rank + states]
    cmat = proj[:, rank + states:]
    uvalue = inner_act.astype(jnp.float32)
    rate = jnp.exp(a_log)
    ssm, final = recurrence(dt, dt * uvalue, bmat, cmat, rate, jnp.zeros_like(rate))
    mixed = (ssm + skip[None, :] * uvalue) * jax.nn.silu(gate_act.astype(jnp.float32))
    return mixed.astype(jnp.bfloat16)
```

```python
import functools
import math

import jax
import jax.numpy as jnp
from jax import lax
from jax.experimental import pallas as pl
from jax.experimental.pallas import tpu as pltpu
from jax.sharding import PartitionSpec as P

LANES = 128
SUB = 8
TILE = LANES * SUB
UNROLL = 8
LOG2E = 1.4426950408889634
F32 = jnp.float32


def softplus(x):
    return jnp.maximum(x, 0.0) + jnp.log1p(jnp.exp(-jnp.abs(x)))


def kernel(seq, mp, tokens, inner, rank, states,
           u_ref, g_ref, xp_ref, dtp_ref, bias_ref, alog_ref, skip_ref, out_ref,
           proj, bs, cs, rate, dts, drv, ys, tot, got, pre, hand, ent,
           mp_send, mp_recv, tot_send, tot_recv, hand_send, hand_recv):
    blocks = pl.cdiv(inner, TILE)
    digit = 4
    stride = seq // digit
    bits = int(math.log2(stride))
    me = lax.axis_index("seq")
    my_mp = lax.axis_index("mp")
    plane = me // stride
    above = lax.rem(me + stride, seq)
    below = lax.rem(me + seq - stride, seq)

    def partner(r):
        bit = lax.rem(me // (1 << r), 2)
        return me + (1 - 2 * bit) * (1 << r), bit

    barrier = pltpu.get_barrier_semaphore()
    for m in range(1, mp):
        pl.semaphore_signal(barrier, inc=1, device_id={"mp": lax.rem(my_mp + m, mp)},
                            device_id_type=pl.DeviceIdType.MESH)
    for r in range(bits):
        pl.semaphore_signal(barrier, inc=1, device_id={"seq": partner(r)[0]},
                            device_id_type=pl.DeviceIdType.MESH)
    for other in (above, below):
        pl.semaphore_signal(barrier, inc=1, device_id={"seq": other},
                            device_id_type=pl.DeviceIdType.MESH)

    proj[my_mp] = jnp.dot(u_ref[...], xp_ref[...], preferred_element_type=F32)
    pl.semaphore_wait(barrier, (mp - 1) + bits + 2)
    shares = []
    for m in range(1, mp):
        copy = pltpu.make_async_remote_copy(
            src_ref=proj.at[my_mp], dst_ref=proj.at[my_mp],
            send_sem=mp_send.at[m - 1], recv_sem=mp_recv.at[m - 1],
            device_id={"mp": lax.rem(my_mp + m, mp)},
            device_id_type=pl.DeviceIdType.MESH)
        copy.start()
        shares.append(copy)

    for k in range(blocks):
        for j in range(min(SUB, inner // LANES - k * SUB)):
            lo = (k * SUB + j) * LANES
            rate[k, pl.ds(j, states, stride=SUB), :] = (
                jnp.exp(alog_ref[:, lo:lo + LANES]) * (-LOG2E))

    for copy in shares:
        copy.wait()
    whole = proj[0]
    for m in range(1, mp):
        whole = whole + proj[m]
    low = whole[:, :rank].astype(jnp.bfloat16)
    for n in range(states):
        bs[n] = jnp.broadcast_to(whole[:, rank + n:rank + n + 1], (tokens, LANES))
        cs[n] = jnp.broadcast_to(
            whole[:, rank + states + n:rank + states + n + 1], (tokens, LANES))

    def lanes_of(k):
        return min(SUB, inner // LANES - k * SUB)

    def steps(k):
        @pl.loop(0, lanes_of(k))
        def _(j):
            lo = pl.multiple_of((k * SUB + j) * LANES, LANES)
            cols = pl.ds(lo, LANES)
            dt = softplus(jnp.dot(low, dtp_ref[:, cols], preferred_element_type=F32)
                          + bias_ref[:, cols])
            dts[k, pl.ds(j, tokens, stride=SUB), :] = dt
            drv[k, pl.ds(j, tokens, stride=SUB), :] = dt * u_ref[:, cols].astype(F32)

    def tile(ref, k, i):
        return ref[k, pl.ds(pl.multiple_of(i * SUB, SUB), SUB), :]

    def scan(k):
        rates = [rate[k, n * SUB:(n + 1) * SUB, :] for n in range(states)]

        def body(it, carry):
            total, hs = carry[0], list(carry[1:])
            for i in range(UNROLL):
                t = it * UNROLL + i
                dt = tile(dts, k, t)
                dr = tile(drv, k, t)
                total = total + dt
                acc = [None, None]
                for n in range(states):
                    b = bs[n, pl.ds(t, 1), :]
                    c = cs[n, pl.ds(t, 1), :]
                    hs[n] = jnp.exp2(rates[n] * dt) * hs[n] + b * dr
                    term = c * hs[n]
                    acc[n % 2] = term if acc[n % 2] is None else acc[n % 2] + term
                ys[k, pl.ds(pl.multiple_of(t * SUB, SUB), SUB), :] = acc[0] + acc[1]
            return (total, *hs)

        zero = jnp.zeros((SUB, LANES), F32)
        final = lax.fori_loop(0, tokens // UNROLL, body, (zero,) * (states + 1))
        for n in range(states):
            tot[0, k, n] = final[1 + n]
            pre[k, n] = zero
        tot[0, k, states] = final[0]
        pre[k, states] = zero

    def exchange(r, k):
        return pltpu.make_async_remote_copy(
            src_ref=tot.at[r, k], dst_ref=got.at[r, k],
            send_sem=tot_send.at[r, k], recv_sem=tot_recv.at[r, k],
            device_id={"seq": partner(r)[0]}, device_id_type=pl.DeviceIdType.MESH)

    def join(r, k):
        bit = partner(r)[1]
        exchange(r, k).wait_recv()
        mine_s = tot[r, k, states]
        theirs_s = got[r, k, states]

        @pl.when(bit == 1)
        def _():
            pre_s = pre[k, states]
            for n in range(states):
                rt = rate[k, n * SUB:(n + 1) * SUB, :]
                theirs = got[r, k, n]
                tot[r + 1, k, n] = jnp.exp2(rt * mine_s) * theirs + tot[r, k, n]
                pre[k, n] = jnp.exp2(rt * pre_s) * theirs + pre[k, n]
            pre[k, states] = pre_s + theirs_s

        @pl.when(bit == 0)
        def _():
            for n in range(states):
                rt = rate[k, n * SUB:(n + 1) * SUB, :]
                tot[r + 1, k, n] = jnp.exp2(rt * theirs_s) * tot[r, k, n] + got[r, k, n]

        tot[r + 1, k, states] = mine_s + theirs_s

    def pass_on(k):
        return pltpu.make_async_remote_copy(
            src_ref=hand.at[0, k], dst_ref=hand.at[1, k],
            send_sem=hand_send.at[k], recv_sem=hand_recv.at[k],
            device_id={"seq": above}, device_id_type=pl.DeviceIdType.MESH)

    def forward(k):
        @pl.when(plane == 0)
        def _():
            for n in range(states):
                hand[0, k, n] = tot[bits, k, n]
                ent[k, n] = pre[k, n]
            pass_on(k).start()

        @pl.when(jnp.logical_and(plane > 0, plane < digit - 1))
        def _():
            pass_on(k).wait_recv()
            all_s = tot[bits, k, states]
            for n in range(states):
                rt = rate[k, n * SUB:(n + 1) * SUB, :]
                hand[0, k, n] = jnp.exp2(rt * all_s) * hand[1, k, n] + tot[bits, k, n]
            pass_on(k).start()

    def enter(k):
        @pl.when(plane == digit - 1)
        def _():
            pass_on(k).wait_recv()

        @pl.when(plane > 0)
        def _():
            pre_s = pre[k, states]
            for n in range(states):
                rt = rate[k, n * SUB:(n + 1) * SUB, :]
                ent[k, n] = jnp.exp2(rt * pre_s) * hand[1, k, n] + pre[k, n]

    def correct(k):
        rates = [rate[k, n * SUB:(n + 1) * SUB, :] for n in range(states)]
        ents = [ent[k, n] for n in range(states)]

        def body(it, total):
            for i in range(UNROLL):
                t = it * UNROLL + i
                total = total + tile(dts, k, t)
                acc = [tile(ys, k, t), None]
                for n in range(states):
                    c = cs[n, pl.ds(t, 1), :]
                    term = c * (jnp.exp2(rates[n] * total) * ents[n])
                    acc[n % 2] = term if acc[n % 2] is None else acc[n % 2] + term
                ys[k, pl.ds(pl.multiple_of(t * SUB, SUB), SUB), :] = acc[0] + acc[1]
            return total

        lax.fori_loop(0, tokens // UNROLL, body, jnp.zeros((SUB, LANES), F32))

    def finish(k):
        @pl.loop(0, lanes_of(k))
        def _(j):
            lo = pl.multiple_of((k * SUB + j) * LANES, LANES)
            cols = pl.ds(lo, LANES)
            y = ys[k, pl.ds(j, tokens, stride=SUB), :]
            g = g_ref[:, cols].astype(F32)
            mixed = (y + skip_ref[:, cols] * u_ref[:, cols].astype(F32)) * (
                g / (1.0 + jnp.exp(-g)))
            out_ref[:, cols] = mixed.astype(out_ref.dtype)

    for step in range(blocks + bits):
        if step < blocks:
            steps(step)
            scan(step)
            exchange(0, step).start()
        for r in range(bits):
            k = step - 1 - r
            if 0 <= k < blocks:
                join(r, k)
                if r + 1 < bits:
                    exchange(r + 1, k).start()
                else:
                    forward(k)
    for k in range(blocks):
        enter(k)
        correct(k)
        finish(k)
    for k in range(blocks):
        for r in range(bits):
            exchange(r, k).wait_send()

        @pl.when(plane < digit - 1)
        def _():
            pass_on(k).wait_send()


def solution(mesh):
    seq, mp = mesh.shape["seq"], mesh.shape["mp"]

    def per_device(inner_act, gate_act, x_proj, dt_proj, dt_bias, a_log, skip):
        tokens, inner = inner_act.shape
        rank, states = dt_proj.shape[0], a_log.shape[0]
        blocks = pl.cdiv(inner, TILE)
        bits = int(math.log2(seq // 4))
        vmem = pl.BlockSpec(memory_space=pltpu.VMEM)
        msg = (states + 1, SUB, LANES)
        return pl.pallas_call(
            functools.partial(kernel, seq, mp, tokens, inner, rank, states),
            out_shape=jax.ShapeDtypeStruct((tokens, inner), jnp.bfloat16),
            in_specs=[vmem] * 7,
            out_specs=vmem,
            scratch_shapes=[
                pltpu.VMEM((mp, tokens, x_proj.shape[1]), F32),
                pltpu.VMEM((states, tokens, LANES), F32),
                pltpu.VMEM((states, tokens, LANES), F32),
                pltpu.VMEM((blocks, states * SUB, LANES), F32),
                pltpu.VMEM((blocks, tokens * SUB, LANES), F32),
                pltpu.VMEM((blocks, tokens * SUB, LANES), F32),
                pltpu.VMEM((blocks, tokens * SUB, LANES), F32),
                pltpu.VMEM((bits + 1, blocks) + msg, F32),
                pltpu.VMEM((bits, blocks) + msg, F32),
                pltpu.VMEM((blocks,) + msg, F32),
                pltpu.VMEM((2, blocks, states, SUB, LANES), F32),
                pltpu.VMEM((blocks, states, SUB, LANES), F32),
                pltpu.SemaphoreType.DMA((mp - 1,)),
                pltpu.SemaphoreType.DMA((mp - 1,)),
                pltpu.SemaphoreType.DMA((bits, blocks)),
                pltpu.SemaphoreType.DMA((bits, blocks)),
                pltpu.SemaphoreType.DMA((blocks,)),
                pltpu.SemaphoreType.DMA((blocks,)),
            ],
            compiler_params=pltpu.CompilerParams(
                collective_id=0, has_side_effects=True,
                vmem_limit_bytes=48 * 1024 * 1024),
        )(inner_act, gate_act, x_proj, dt_proj, dt_bias.reshape(1, inner), a_log,
          skip.reshape(1, inner))

    placed = (
        P("seq", "mp"),
        P("seq", "mp"),
        P("mp", None),
        P(None, "mp"),
        P("mp"),
        P(None, "mp"),
        P("mp"),
    )
    return jax.shard_map(
        per_device, mesh=mesh, in_specs=placed, out_specs=P("seq", "mp"), check_vma=False
    )
```

```python
import functools

import jax
import jax.numpy as jnp
from jax import lax
from jax.experimental import pallas as pl
from jax.experimental.pallas import tpu as pltpu
from jax.sharding import PartitionSpec as P

LANES = 128
SUB = 8
TILE = LANES * SUB
UNROLL = 8
LOG2E = 1.4426950408889634
F32 = jnp.float32


def softplus(x):
    e = jnp.exp(-jnp.abs(x))
    series = e * (1.0 - e * (0.5 - e * (1.0 / 3.0 - e * (0.25 - e * 0.2))))
    return jnp.maximum(x, 0.0) + jnp.where(e < 0.03125, series, jnp.log(1.0 + e))


def kernel(seq, mp, tokens, inner, rank, states,
           u_hbm, g_hbm, xp_hbm, dtp_hbm, bias_hbm, alog_hbm, skip_hbm, out_ref,
           u_ref, g_ref, xp_ref, dtp_ref, bias_ref, alog_ref, skip_ref,
           proj, bs, cs, rate, raw, dts, drv, ys, tot, sums, got_e, got_s, back, ent, far, near,
           in_sem, mp_send, mp_recv, e_send, e_recv, s_send, s_recv, b_send, b_recv,
           f_send, f_recv):
    blocks = pl.cdiv(inner, TILE)
    group = states
    groups = seq // group
    me = lax.axis_index("seq")
    my_mp = lax.axis_index("mp")
    mine = lax.rem(me, group)
    my_group = me // group
    base = my_group * group

    loads = [pltpu.make_async_copy(src, dst, in_sem.at[i]) for i, (src, dst) in enumerate((
        (u_hbm, u_ref), (xp_hbm, xp_ref), (alog_hbm, alog_ref), (dtp_hbm, dtp_ref),
        (bias_hbm, bias_ref), (g_hbm, g_ref), (skip_hbm, skip_ref)))]
    for load in loads:
        load.start()

    barrier = pltpu.get_barrier_semaphore()
    for m in range(1, mp):
        pl.semaphore_signal(barrier, inc=1, device_id={"mp": lax.rem(my_mp + m, mp)},
                            device_id_type=pl.DeviceIdType.MESH)
    for p in range(1, group):
        pl.semaphore_signal(barrier, inc=1,
                            device_id={"seq": base + lax.rem(mine + p, group)},
                            device_id_type=pl.DeviceIdType.MESH)
    for p in range(1, groups):
        pl.semaphore_signal(barrier, inc=1, device_id={"seq": lax.rem(me + p * group, seq)},
                            device_id_type=pl.DeviceIdType.MESH)

    loads[0].wait()
    loads[1].wait()
    proj[my_mp] = lax.dot_general(u_ref[...], xp_ref[...], (((1,), (1,)), ((), ())),
                                  preferred_element_type=F32)
    pl.semaphore_wait(barrier, (mp - 1) + (group - 1) + (groups - 1))
    shares = []
    for m in range(1, mp):
        copy = pltpu.make_async_remote_copy(
            src_ref=proj.at[my_mp], dst_ref=proj.at[my_mp],
            send_sem=mp_send.at[m - 1], recv_sem=mp_recv.at[m - 1],
            device_id={"mp": lax.rem(my_mp + m, mp)},
            device_id_type=pl.DeviceIdType.MESH)
        copy.start()
        shares.append(copy)

    loads[2].wait()
    for k in range(blocks):
        for j in range(min(SUB, inner // LANES - k * SUB)):
            lo = (k * SUB + j) * LANES
            rate[k, pl.ds(j, states, stride=SUB), :] = (
                jnp.exp(alog_ref[:, lo:lo + LANES]) * (-LOG2E))
    loads[3].wait()
    loads[4].wait()

    for copy in shares:
        copy.wait()
    whole = proj[0]
    for m in range(1, mp):
        whole = whole + proj[m]
    low = whole[:, :rank].astype(jnp.bfloat16)

    def lanes_of(k):
        return min(SUB, inner // LANES - k * SUB)

    def tile(ref, k, i):
        return ref[k, pl.ds(pl.multiple_of(i * SUB, SUB), SUB), :]

    def steps(k):
        width = lanes_of(k) * LANES
        raw[:, :width] = jnp.dot(low, dtp_ref[:, k * TILE:k * TILE + width],
                                 preferred_element_type=F32)
        @pl.loop(0, lanes_of(k))
        def _(j):
            lo = pl.multiple_of((k * SUB + j) * LANES, LANES)
            cols = pl.ds(lo, LANES)
            dt = softplus(raw[:, pl.ds(pl.multiple_of(j * LANES, LANES), LANES)]
                          + bias_ref[:, cols])
            dts[k, pl.ds(j, tokens, stride=SUB), :] = dt
            drv[k, pl.ds(j, tokens, stride=SUB), :] = dt * u_ref[:, cols].astype(F32)
            sums[k, pl.ds(j, 1), :] = jnp.sum(dt, axis=0, keepdims=True)

        got_s[k, 0] = sums[k]

        @pl.loop(1, group)
        def _(p):
            pltpu.make_async_remote_copy(
                src_ref=sums.at[k], dst_ref=got_s.at[k, group - p],
                send_sem=s_send.at[k], recv_sem=s_recv.at[k],
                device_id={"seq": base + lax.rem(mine + p, group)},
                device_id_type=pl.DeviceIdType.MESH).start()

    def scan(k):
        rates = [rate[k, n * SUB:(n + 1) * SUB, :] for n in range(states)]

        def body(it, hs):
            hs = list(hs)
            for i in range(UNROLL):
                t = it * UNROLL + i
                dt = tile(dts, k, t)
                dr = tile(drv, k, t)
                acc = [None, None]
                for n in range(states):
                    b = bs[n, pl.ds(t, 1), :]
                    c = cs[n, pl.ds(t, 1), :]
                    hs[n] = jnp.exp2(rates[n] * dt) * hs[n] + b * dr
                    term = c * hs[n]
                    acc[n % 2] = term if acc[n % 2] is None else acc[n % 2] + term
                ys[k, pl.ds(pl.multiple_of(t * SUB, SUB), SUB), :] = acc[0] + acc[1]
            return tuple(hs)

        zero = jnp.zeros((SUB, LANES), F32)
        final = lax.fori_loop(0, tokens // UNROLL, body, (zero,) * states)
        for n in range(states):
            tot[k, n] = final[n]
        got_e[k, 0] = tot[k, mine]

        @pl.loop(1, group)
        def _(p):
            owner = lax.rem(mine + p, group)
            pltpu.make_async_remote_copy(
                src_ref=tot.at[k, owner], dst_ref=got_e.at[k, group - p],
                send_sem=e_send.at[k], recv_sem=e_recv.at[k],
                device_id={"seq": base + owner},
                device_id_type=pl.DeviceIdType.MESH).start()

    def drain(ref, k, sem):
        part = ref.at[k, pl.ds(1, group - 1)]
        pltpu.make_async_copy(part, part, sem.at[k]).wait()

    def own(k):
        drain(got_s, k, s_recv)
        drain(got_e, k, e_recv)
        rt = rate[k, pl.ds(pl.multiple_of(mine * SUB, SUB), SUB), :]
        slots = [lax.rem(j - mine + group, group) for j in range(group)]
        carry = jnp.zeros((SUB, LANES), F32)
        if groups > 1:
            end, span = carry, carry
            for slot in slots:
                end = jnp.exp2(rt * got_s[k, slot]) * end + got_e[k, slot]
                span = span + got_s[k, slot]
            near[k, 0] = end
            near[k, 1] = span
            sent = [pltpu.make_async_remote_copy(
                src_ref=near.at[k], dst_ref=far.at[k, groups - p],
                send_sem=f_send.at[k, p], recv_sem=f_recv.at[k, groups - p],
                device_id={"seq": lax.rem(me + p * group, seq)},
                device_id_type=pl.DeviceIdType.MESH) for p in range(1, groups)]
            for copy in sent:
                copy.start()
            for copy in sent:
                copy.wait()
            far[k, 0] = near[k]
            for g in range(groups - 1):
                slot = lax.rem(g - my_group + groups, groups)
                carry = jnp.where(
                    g < my_group, jnp.exp2(rt * far[k, slot, 1]) * carry + far[k, slot, 0], carry)
        for slot in slots:
            back[k, slot] = carry
            carry = jnp.exp2(rt * got_s[k, slot]) * carry + got_e[k, slot]
        ent[k, 0] = back[k, 0]

        @pl.loop(1, group)
        def _(p):
            pltpu.make_async_remote_copy(
                src_ref=back.at[k, p], dst_ref=ent.at[k, group - p],
                send_sem=b_send.at[k], recv_sem=b_recv.at[k],
                device_id={"seq": base + lax.rem(mine + p, group)},
                device_id_type=pl.DeviceIdType.MESH).start()

    def correct(k):
        drain(ent, k, b_recv)
        rates = [rate[k, n * SUB:(n + 1) * SUB, :] for n in range(states)]
        ents = [ent[k, lax.rem(n - mine + group, group)] for n in range(states)]

        def body(it, total):
            for i in range(UNROLL):
                t = it * UNROLL + i
                total = total + tile(dts, k, t)
                acc = [tile(ys, k, t), None]
                for n in range(states):
                    c = cs[n, pl.ds(t, 1), :]
                    term = c * (jnp.exp2(rates[n] * total) * ents[n])
                    acc[n % 2] = term if acc[n % 2] is None else acc[n % 2] + term
                ys[k, pl.ds(pl.multiple_of(t * SUB, SUB), SUB), :] = acc[0] + acc[1]
            return total

        lax.fori_loop(0, tokens // UNROLL, body, jnp.zeros((SUB, LANES), F32))

    def finish(k):
        @pl.loop(0, lanes_of(k))
        def _(j):
            lo = pl.multiple_of((k * SUB + j) * LANES, LANES)
            cols = pl.ds(lo, LANES)
            y = ys[k, pl.ds(j, tokens, stride=SUB), :]
            g = g_ref[:, cols].astype(F32)
            mixed = (y + skip_ref[:, cols] * u_ref[:, cols].astype(F32)) * (
                g / (1.0 + jnp.exp(-g)))
            out_ref[:, cols] = mixed.astype(out_ref.dtype)

    if inner % TILE:
        sums[blocks - 1] = jnp.zeros((SUB, LANES), F32)
    for k in range(blocks):
        steps(k)
    for n in range(states):
        bs[n] = jnp.broadcast_to(whole[:, rank + n:rank + n + 1], (tokens, LANES))
        cs[n] = jnp.broadcast_to(
            whole[:, rank + states + n:rank + states + n + 1], (tokens, LANES))
    for k in range(blocks):
        scan(k)
        if k > 0:
            own(k - 1)
    loads[5].wait()
    loads[6].wait()
    for k in range(blocks - 1):
        correct(k)
        finish(k)
        if k == 0:
            own(blocks - 1)
    if blocks == 1:
        own(0)
    correct(blocks - 1)
    finish(blocks - 1)
    for k in range(blocks):
        drain(got_s, k, s_send)
        drain(got_e, k, e_send)
        drain(back, k, b_send)


def solution(mesh):
    seq, mp = mesh.shape["seq"], mesh.shape["mp"]

    def per_device(inner_act, gate_act, x_proj, dt_proj, dt_bias, a_log, skip):
        tokens, inner = inner_act.shape
        rank, states = dt_proj.shape[0], a_log.shape[0]
        blocks = pl.cdiv(inner, TILE)
        group, groups = states, seq // states
        hbm = pl.BlockSpec(memory_space=pltpu.MemorySpace.HBM)
        args = (inner_act, gate_act, x_proj.T, dt_proj, dt_bias.reshape(1, inner), a_log,
                skip.reshape(1, inner))
        cell = (SUB, LANES)
        dma = pltpu.SemaphoreType.DMA
        return pl.pallas_call(
            functools.partial(kernel, seq, mp, tokens, inner, rank, states),
            out_shape=jax.ShapeDtypeStruct((tokens, inner), jnp.bfloat16),
            in_specs=[hbm] * len(args),
            out_specs=pl.BlockSpec(memory_space=pltpu.VMEM),
            scratch_shapes=[pltpu.VMEM(a.shape, a.dtype) for a in args] + [
                pltpu.VMEM((mp, tokens, x_proj.shape[1]), F32),
                pltpu.VMEM((states, tokens, LANES), F32),
                pltpu.VMEM((states, tokens, LANES), F32),
                pltpu.VMEM((blocks, states * SUB, LANES), F32),
                pltpu.VMEM((tokens, TILE), F32),
                pltpu.VMEM((blocks, tokens * SUB, LANES), F32),
                pltpu.VMEM((blocks, tokens * SUB, LANES), F32),
                pltpu.VMEM((blocks, tokens * SUB, LANES), F32),
                pltpu.VMEM((blocks, states) + cell, F32),
                pltpu.VMEM((blocks,) + cell, F32),
                pltpu.VMEM((blocks, group) + cell, F32),
                pltpu.VMEM((blocks, group) + cell, F32),
                pltpu.VMEM((blocks, group) + cell, F32),
                pltpu.VMEM((blocks, group) + cell, F32),
                pltpu.VMEM((blocks, groups, 2) + cell, F32),
                pltpu.VMEM((blocks, 2) + cell, F32),
                dma((len(args),)),
                dma((mp - 1,)), dma((mp - 1,)),
                dma((blocks,)), dma((blocks,)),
                dma((blocks,)), dma((blocks,)),
                dma((blocks,)), dma((blocks,)),
                dma((blocks, groups)), dma((blocks, groups)),
            ],
            compiler_params=pltpu.CompilerParams(
                collective_id=0, has_side_effects=True,
                vmem_limit_bytes=48 * 1024 * 1024),
        )(*args)

    placed = (
        P("seq", "mp"),
        P("seq", "mp"),
        P("mp", None),
        P(None, "mp"),
        P("mp"),
        P(None, "mp"),
        P("mp"),
    )
    return jax.shard_map(
        per_device, mesh=mesh, in_specs=placed, out_specs=P("seq", "mp"), check_vma=False
    )
```

```python
import functools

import jax
import jax.numpy as jnp
from jax import lax
from jax.experimental import pallas as pl
from jax.experimental.pallas import tpu as pltpu
from jax.sharding import PartitionSpec as P

LANES = 128
SUB = 8
TILE = LANES * SUB
UNROLL = 8
LOG2E = 1.4426950408889634
F32 = jnp.float32


def softplus(x):
    e = jnp.exp(-jnp.abs(x))
    series = e * (1.0 - e * (0.5 - e * (1.0 / 3.0 - e * (0.25 - e * 0.2))))
    return jnp.maximum(x, 0.0) + jnp.where(e < 0.03125, series, jnp.log(1.0 + e))


def kernel(seq, mp, tokens, inner, rank, states,
           u_hbm, g_hbm, xp_hbm, dtp_hbm, bias_hbm, alog_hbm, skip_hbm, out_ref,
           u_ref, g_ref, xp_ref, dtp_ref, bias_ref, alog_ref, skip_ref,
           proj, bs, cs, rate, raw, dts, drv, ys, fades, tot, sums, got_e, got_s, back, ent, far, near,
           in_sem, mp_send, mp_recv, e_send, e_recv, s_send, s_recv, b_send, b_recv,
           f_send, f_recv):
    blocks = pl.cdiv(inner, TILE)
    group = states
    groups = seq // group
    me = lax.axis_index("seq")
    my_mp = lax.axis_index("mp")
    mine = lax.rem(me, group)
    my_group = me // group
    base = my_group * group

    loads = [pltpu.make_async_copy(src, dst, in_sem.at[i]) for i, (src, dst) in enumerate((
        (u_hbm, u_ref), (xp_hbm, xp_ref), (alog_hbm, alog_ref), (dtp_hbm, dtp_ref),
        (bias_hbm, bias_ref), (g_hbm, g_ref), (skip_hbm, skip_ref)))]
    for load in loads:
        load.start()

    barrier = pltpu.get_barrier_semaphore()
    for m in range(1, mp):
        pl.semaphore_signal(barrier, inc=1, device_id={"mp": lax.rem(my_mp + m, mp)},
                            device_id_type=pl.DeviceIdType.MESH)
    for p in range(1, group):
        pl.semaphore_signal(barrier, inc=1,
                            device_id={"seq": base + lax.rem(mine + p, group)},
                            device_id_type=pl.DeviceIdType.MESH)
    for p in range(1, groups):
        pl.semaphore_signal(barrier, inc=1, device_id={"seq": lax.rem(me + p * group, seq)},
                            device_id_type=pl.DeviceIdType.MESH)

    loads[0].wait()
    loads[1].wait()
    proj[my_mp] = lax.dot_general(u_ref[...], xp_ref[...], (((1,), (1,)), ((), ())),
                                  preferred_element_type=F32)
    pl.semaphore_wait(barrier, (mp - 1) + (group - 1) + (groups - 1))
    shares = []
    for m in range(1, mp):
        copy = pltpu.make_async_remote_copy(
            src_ref=proj.at[my_mp], dst_ref=proj.at[my_mp],
            send_sem=mp_send.at[m - 1], recv_sem=mp_recv.at[m - 1],
            device_id={"mp": lax.rem(my_mp + m, mp)},
            device_id_type=pl.DeviceIdType.MESH)
        copy.start()
        shares.append(copy)

    loads[2].wait()
    for k in range(blocks):
        for j in range(min(SUB, inner // LANES - k * SUB)):
            lo = (k * SUB + j) * LANES
            rate[k, pl.ds(j, states, stride=SUB), :] = (
                jnp.exp(alog_ref[:, lo:lo + LANES]) * (-LOG2E))
    loads[3].wait()
    loads[4].wait()

    for copy in shares:
        copy.wait()
    whole = proj[0]
    for m in range(1, mp):
        whole = whole + proj[m]
    low = whole[:, :rank].astype(jnp.bfloat16)

    def lanes_of(k):
        return min(SUB, inner // LANES - k * SUB)

    def tile(ref, k, i):
        return ref[k, pl.ds(pl.multiple_of(i * SUB, SUB), SUB), :]

    def steps(k):
        width = lanes_of(k) * LANES
        raw[:, :width] = jnp.dot(low, dtp_ref[:, k * TILE:k * TILE + width],
                                 preferred_element_type=F32)
        @pl.loop(0, lanes_of(k))
        def _(j):
            lo = pl.multiple_of((k * SUB + j) * LANES, LANES)
            cols = pl.ds(lo, LANES)
            dt = softplus(raw[:, pl.ds(pl.multiple_of(j * LANES, LANES), LANES)]
                          + bias_ref[:, cols])
            dts[k, pl.ds(j, tokens, stride=SUB), :] = dt
            drv[k, pl.ds(j, tokens, stride=SUB), :] = dt * u_ref[:, cols].astype(F32)
            sums[k, pl.ds(j, 1), :] = jnp.sum(dt, axis=0, keepdims=True)

        got_s[k, 0] = sums[k]

        @pl.loop(1, group)
        def _(p):
            pltpu.make_async_remote_copy(
                src_ref=sums.at[k], dst_ref=got_s.at[k, group - p],
                send_sem=s_send.at[k], recv_sem=s_recv.at[k],
                device_id={"seq": base + lax.rem(mine + p, group)},
                device_id_type=pl.DeviceIdType.MESH).start()

    def cell(t, n):
        return pl.ds(pl.multiple_of((t * states + n) * SUB, SUB), SUB)

    def ends(k):
        rates = [rate[k, n * SUB:(n + 1) * SUB, :] for n in range(states)]

        def body(it, hs):
            hs = list(hs)
            for i in range(UNROLL):
                t = it * UNROLL + i
                dt = tile(dts, k, t)
                dr = tile(drv, k, t)
                for n in range(states):
                    fade = jnp.exp2(rates[n] * dt)
                    fades[k, cell(t, n), :] = fade
                    hs[n] = fade * hs[n] + bs[n, pl.ds(t, 1), :] * dr
            return tuple(hs)

        zero = jnp.zeros((SUB, LANES), F32)
        final = lax.fori_loop(0, tokens // UNROLL, body, (zero,) * states)
        for n in range(states):
            tot[k, n] = final[n]
        got_e[k, 0] = tot[k, mine]

        @pl.loop(1, group)
        def _(p):
            owner = lax.rem(mine + p, group)
            pltpu.make_async_remote_copy(
                src_ref=tot.at[k, owner], dst_ref=got_e.at[k, group - p],
                send_sem=e_send.at[k], recv_sem=e_recv.at[k],
                device_id={"seq": base + owner},
                device_id_type=pl.DeviceIdType.MESH).start()

    def local(k):
        def body(it, hs):
            hs = list(hs)
            for i in range(UNROLL):
                t = it * UNROLL + i
                dr = tile(drv, k, t)
                acc = [None, None]
                for n in range(states):
                    hs[n] = fades[k, cell(t, n), :] * hs[n] + bs[n, pl.ds(t, 1), :] * dr
                    term = cs[n, pl.ds(t, 1), :] * hs[n]
                    acc[n % 2] = term if acc[n % 2] is None else acc[n % 2] + term
                ys[k, pl.ds(pl.multiple_of(t * SUB, SUB), SUB), :] = acc[0] + acc[1]
            return tuple(hs)

        zero = jnp.zeros((SUB, LANES), F32)
        lax.fori_loop(0, tokens // UNROLL, body, (zero,) * states)

    def drain(ref, k, sem):
        part = ref.at[k, pl.ds(1, group - 1)]
        pltpu.make_async_copy(part, part, sem.at[k]).wait()

    def own(k):
        drain(got_s, k, s_recv)
        drain(got_e, k, e_recv)
        rt = rate[k, pl.ds(pl.multiple_of(mine * SUB, SUB), SUB), :]
        slots = [lax.rem(j - mine + group, group) for j in range(group)]
        carry = jnp.zeros((SUB, LANES), F32)
        if groups > 1:
            end, span = carry, carry
            for slot in slots:
                end = jnp.exp2(rt * got_s[k, slot]) * end + got_e[k, slot]
                span = span + got_s[k, slot]
            near[k, 0] = end
            near[k, 1] = span
            sent = [pltpu.make_async_remote_copy(
                src_ref=near.at[k], dst_ref=far.at[k, groups - p],
                send_sem=f_send.at[k, p], recv_sem=f_recv.at[k, groups - p],
                device_id={"seq": lax.rem(me + p * group, seq)},
                device_id_type=pl.DeviceIdType.MESH) for p in range(1, groups)]
            for copy in sent:
                copy.start()
            for copy in sent:
                copy.wait()
            far[k, 0] = near[k]
            for g in range(groups - 1):
                slot = lax.rem(g - my_group + groups, groups)
                carry = jnp.where(
                    g < my_group, jnp.exp2(rt * far[k, slot, 1]) * carry + far[k, slot, 0], carry)
        for slot in slots:
            back[k, slot] = carry
            carry = jnp.exp2(rt * got_s[k, slot]) * carry + got_e[k, slot]
        ent[k, 0] = back[k, 0]

        @pl.loop(1, group)
        def _(p):
            pltpu.make_async_remote_copy(
                src_ref=back.at[k, p], dst_ref=ent.at[k, group - p],
                send_sem=b_send.at[k], recv_sem=b_recv.at[k],
                device_id={"seq": base + lax.rem(mine + p, group)},
                device_id_type=pl.DeviceIdType.MESH).start()

    def correct(k):
        drain(ent, k, b_recv)
        ents = [ent[k, lax.rem(n - mine + group, group)] for n in range(states)]

        def body(it, es):
            es = list(es)
            for i in range(UNROLL):
                t = it * UNROLL + i
                acc = [tile(ys, k, t), None]
                for n in range(states):
                    es[n] = fades[k, cell(t, n), :] * es[n]
                    term = cs[n, pl.ds(t, 1), :] * es[n]
                    acc[n % 2] = term if acc[n % 2] is None else acc[n % 2] + term
                ys[k, pl.ds(pl.multiple_of(t * SUB, SUB), SUB), :] = acc[0] + acc[1]
            return tuple(es)

        lax.fori_loop(0, tokens // UNROLL, body, tuple(ents))

    def finish(k):
        @pl.loop(0, lanes_of(k))
        def _(j):
            lo = pl.multiple_of((k * SUB + j) * LANES, LANES)
            cols = pl.ds(lo, LANES)
            y = ys[k, pl.ds(j, tokens, stride=SUB), :]
            g = g_ref[:, cols].astype(F32)
            mixed = (y + skip_ref[:, cols] * u_ref[:, cols].astype(F32)) * (
                g / (1.0 + jnp.exp(-g)))
            out_ref[:, cols] = mixed.astype(out_ref.dtype)

    if inner % TILE:
        sums[blocks - 1] = jnp.zeros((SUB, LANES), F32)
    for k in range(blocks):
        steps(k)
    for n in range(states):
        bs[n] = jnp.broadcast_to(whole[:, rank + n:rank + n + 1], (tokens, LANES))
    for k in range(blocks):
        ends(k)
    for n in range(states):
        cs[n] = jnp.broadcast_to(
            whole[:, rank + states + n:rank + states + n + 1], (tokens, LANES))
    for k in range(blocks):
        local(k)
        own(k)
    loads[5].wait()
    loads[6].wait()
    for k in range(blocks):
        correct(k)
        finish(k)
    for k in range(blocks):
        drain(got_s, k, s_send)
        drain(got_e, k, e_send)
        drain(back, k, b_send)


def solution(mesh):
    seq, mp = mesh.shape["seq"], mesh.shape["mp"]

    def per_device(inner_act, gate_act, x_proj, dt_proj, dt_bias, a_log, skip):
        tokens, inner = inner_act.shape
        rank, states = dt_proj.shape[0], a_log.shape[0]
        blocks = pl.cdiv(inner, TILE)
        group, groups = states, seq // states
        hbm = pl.BlockSpec(memory_space=pltpu.MemorySpace.HBM)
        args = (inner_act, gate_act, x_proj.T, dt_proj, dt_bias.reshape(1, inner), a_log,
                skip.reshape(1, inner))
        cell = (SUB, LANES)
        dma = pltpu.SemaphoreType.DMA
        return pl.pallas_call(
            functools.partial(kernel, seq, mp, tokens, inner, rank, states),
            out_shape=jax.ShapeDtypeStruct((tokens, inner), jnp.bfloat16),
            in_specs=[hbm] * len(args),
            out_specs=pl.BlockSpec(memory_space=pltpu.VMEM),
            scratch_shapes=[pltpu.VMEM(a.shape, a.dtype) for a in args] + [
                pltpu.VMEM((mp, tokens, x_proj.shape[1]), F32),
                pltpu.VMEM((states, tokens, LANES), F32),
                pltpu.VMEM((states, tokens, LANES), F32),
                pltpu.VMEM((blocks, states * SUB, LANES), F32),
                pltpu.VMEM((tokens, TILE), F32),
                pltpu.VMEM((blocks, tokens * SUB, LANES), F32),
                pltpu.VMEM((blocks, tokens * SUB, LANES), F32),
                pltpu.VMEM((blocks, tokens * SUB, LANES), F32),
                pltpu.VMEM((blocks, tokens * states * SUB, LANES), F32),
                pltpu.VMEM((blocks, states) + cell, F32),
                pltpu.VMEM((blocks,) + cell, F32),
                pltpu.VMEM((blocks, group) + cell, F32),
                pltpu.VMEM((blocks, group) + cell, F32),
                pltpu.VMEM((blocks, group) + cell, F32),
                pltpu.VMEM((blocks, group) + cell, F32),
                pltpu.VMEM((blocks, groups, 2) + cell, F32),
                pltpu.VMEM((blocks, 2) + cell, F32),
                dma((len(args),)),
                dma((mp - 1,)), dma((mp - 1,)),
                dma((blocks,)), dma((blocks,)),
                dma((blocks,)), dma((blocks,)),
                dma((blocks,)), dma((blocks,)),
                dma((blocks, groups)), dma((blocks, groups)),
            ],
            compiler_params=pltpu.CompilerParams(
                collective_id=0, has_side_effects=True,
                vmem_limit_bytes=62 * 1024 * 1024),
        )(*args)

    placed = (
        P("seq", "mp"),
        P("seq", "mp"),
        P("mp", None),
        P(None, "mp"),
        P("mp"),
        P(None, "mp"),
        P("mp"),
    )
    return jax.shard_map(
        per_device, mesh=mesh, in_specs=placed, out_specs=P("seq", "mp"), check_vma=False
    )
```

```python
import functools

import jax
import jax.numpy as jnp
from jax import lax
from jax.experimental import pallas as pl
from jax.experimental.pallas import tpu as pltpu
from jax.sharding import PartitionSpec as P

LANES = 128
SUB = 8
TILE = LANES * SUB
UNROLL = 8
LOG2E = 1.4426950408889634
F32 = jnp.float32


def softplus(x):
    e = jnp.exp(-jnp.abs(x))
    series = e * (1.0 - e * (0.5 - e * (1.0 / 3.0 - e * (0.25 - e * 0.2))))
    return jnp.maximum(x, 0.0) + jnp.where(e < 0.03125, series, jnp.log(1.0 + e))


def kernel(seq, mp, tokens, inner, rank, states,
           u_hbm, g_hbm, xp_hbm, dtp_hbm, bias_hbm, alog_hbm, skip_hbm, out_ref,
           u_ref, g_ref, xp_ref, dtp_ref, bias_ref, alog_ref, skip_ref,
           proj, bs, cs, rate, raw, dts, drv, ys, fades, tot, sums, got_e, got_s, back, ent, far, near,
           in_sem, mp_send, mp_recv, e_send, e_recv, s_send, s_recv, b_send, b_recv,
           f_send, f_recv):
    blocks = pl.cdiv(inner, TILE)
    group = states
    groups = seq // group
    me = lax.axis_index("seq")
    my_mp = lax.axis_index("mp")
    mine = lax.rem(me, group)
    my_group = me // group
    base = my_group * group

    loads = [pltpu.make_async_copy(src, dst, in_sem.at[i]) for i, (src, dst) in enumerate((
        (u_hbm, u_ref), (xp_hbm, xp_ref), (alog_hbm, alog_ref), (dtp_hbm, dtp_ref),
        (bias_hbm, bias_ref), (g_hbm, g_ref), (skip_hbm, skip_ref)))]
    for load in loads:
        load.start()

    barrier = pltpu.get_barrier_semaphore()
    for m in range(1, mp):
        pl.semaphore_signal(barrier, inc=1, device_id={"mp": lax.rem(my_mp + m, mp)},
                            device_id_type=pl.DeviceIdType.MESH)
    for p in range(1, group):
        pl.semaphore_signal(barrier, inc=1,
                            device_id={"seq": base + lax.rem(mine + p, group)},
                            device_id_type=pl.DeviceIdType.MESH)
    for p in range(1, groups):
        pl.semaphore_signal(barrier, inc=1, device_id={"seq": lax.rem(me + p * group, seq)},
                            device_id_type=pl.DeviceIdType.MESH)

    loads[0].wait()
    loads[1].wait()
    proj[my_mp] = lax.dot_general(u_ref[...], xp_ref[...], (((1,), (1,)), ((), ())),
                                  preferred_element_type=F32)
    pl.semaphore_wait(barrier, (mp - 1) + (group - 1) + (groups - 1))
    shares = []
    for m in range(1, mp):
        copy = pltpu.make_async_remote_copy(
            src_ref=proj.at[my_mp], dst_ref=proj.at[my_mp],
            send_sem=mp_send.at[m - 1], recv_sem=mp_recv.at[m - 1],
            device_id={"mp": lax.rem(my_mp + m, mp)},
            device_id_type=pl.DeviceIdType.MESH)
        copy.start()
        shares.append(copy)

    loads[2].wait()
    for k in range(blocks):
        for j in range(min(SUB, inner // LANES - k * SUB)):
            lo = (k * SUB + j) * LANES
            rate[k, pl.ds(j, states, stride=SUB), :] = (
                jnp.exp(alog_ref[:, lo:lo + LANES]) * (-LOG2E))
    loads[3].wait()
    loads[4].wait()

    for copy in shares:
        copy.wait()
    whole = proj[0]
    for m in range(1, mp):
        whole = whole + proj[m]
    low = whole[:, :rank].astype(jnp.bfloat16)

    def lanes_of(k):
        return min(SUB, inner // LANES - k * SUB)

    def tile(ref, k, i):
        return ref[k, pl.ds(pl.multiple_of(i * SUB, SUB), SUB), :]

    def steps(k):
        width = lanes_of(k) * LANES
        raw[:, :width] = jnp.dot(low, dtp_ref[:, k * TILE:k * TILE + width],
                                 preferred_element_type=F32)
        @pl.loop(0, lanes_of(k))
        def _(j):
            lo = pl.multiple_of((k * SUB + j) * LANES, LANES)
            cols = pl.ds(lo, LANES)
            dt = softplus(raw[:, pl.ds(pl.multiple_of(j * LANES, LANES), LANES)]
                          + bias_ref[:, cols])
            dts[k, pl.ds(j, tokens, stride=SUB), :] = dt
            drv[k, pl.ds(j, tokens, stride=SUB), :] = dt * u_ref[:, cols].astype(F32)
            sums[k, pl.ds(j, 1), :] = jnp.sum(dt, axis=0, keepdims=True)

        got_s[k, 0] = sums[k]

        @pl.loop(1, group)
        def _(p):
            pltpu.make_async_remote_copy(
                src_ref=sums.at[k], dst_ref=got_s.at[k, group - p],
                send_sem=s_send.at[k], recv_sem=s_recv.at[k],
                device_id={"seq": base + lax.rem(mine + p, group)},
                device_id_type=pl.DeviceIdType.MESH).start()

    def cell(t, n):
        return pl.ds(pl.multiple_of((t * states + n) * SUB, SUB), SUB)

    def ends(k):
        rates = [rate[k, n * SUB:(n + 1) * SUB, :] for n in range(states)]

        def body(it, hs):
            hs = list(hs)
            for i in range(UNROLL):
                t = it * UNROLL + i
                dt = tile(dts, k, t)
                dr = tile(drv, k, t)
                for n in range(states):
                    fade = jnp.exp2(rates[n] * dt)
                    fades[k, cell(t, n), :] = fade
                    hs[n] = fade * hs[n] + bs[n, pl.ds(t, 1), :] * dr
            return tuple(hs)

        zero = jnp.zeros((SUB, LANES), F32)
        final = lax.fori_loop(0, tokens // UNROLL, body, (zero,) * states)
        for n in range(states):
            tot[k, n] = final[n]
        got_e[k, 0] = tot[k, mine]

        @pl.loop(1, group)
        def _(p):
            owner = lax.rem(mine + p, group)
            pltpu.make_async_remote_copy(
                src_ref=tot.at[k, owner], dst_ref=got_e.at[k, group - p],
                send_sem=e_send.at[k], recv_sem=e_recv.at[k],
                device_id={"seq": base + owner},
                device_id_type=pl.DeviceIdType.MESH).start()

    def local(k):
        def body(it, hs):
            hs = list(hs)
            for i in range(UNROLL):
                t = it * UNROLL + i
                dr = tile(drv, k, t)
                acc = [None, None]
                for n in range(states):
                    hs[n] = fades[k, cell(t, n), :] * hs[n] + bs[n, pl.ds(t, 1), :] * dr
                    term = cs[n, pl.ds(t, 1), :] * hs[n]
                    acc[n % 2] = term if acc[n % 2] is None else acc[n % 2] + term
                ys[k, pl.ds(pl.multiple_of(t * SUB, SUB), SUB), :] = acc[0] + acc[1]
            return tuple(hs)

        zero = jnp.zeros((SUB, LANES), F32)
        lax.fori_loop(0, tokens // UNROLL, body, (zero,) * states)

    def drain(ref, k, sem):
        part = ref.at[k, pl.ds(1, group - 1)]
        pltpu.make_async_copy(part, part, sem.at[k]).wait()

    def own(k):
        drain(got_s, k, s_recv)
        drain(got_e, k, e_recv)
        rt = rate[k, pl.ds(pl.multiple_of(mine * SUB, SUB), SUB), :]
        slots = [lax.rem(j - mine + group, group) for j in range(group)]
        carry = jnp.zeros((SUB, LANES), F32)
        if groups > 1:
            end, span = carry, carry
            for slot in slots:
                end = jnp.exp2(rt * got_s[k, slot]) * end + got_e[k, slot]
                span = span + got_s[k, slot]
            near[k, 0] = end
            near[k, 1] = span
            sent = [pltpu.make_async_remote_copy(
                src_ref=near.at[k], dst_ref=far.at[k, groups - p],
                send_sem=f_send.at[k, p], recv_sem=f_recv.at[k, groups - p],
                device_id={"seq": lax.rem(me + p * group, seq)},
                device_id_type=pl.DeviceIdType.MESH) for p in range(1, groups)]
            for copy in sent:
                copy.start()
            for copy in sent:
                copy.wait()
            far[k, 0] = near[k]
            for g in range(groups - 1):
                slot = lax.rem(g - my_group + groups, groups)
                carry = jnp.where(
                    g < my_group, jnp.exp2(rt * far[k, slot, 1]) * carry + far[k, slot, 0], carry)
        for slot in slots:
            back[k, slot] = carry
            carry = jnp.exp2(rt * got_s[k, slot]) * carry + got_e[k, slot]
        ent[k, 0] = back[k, 0]

        @pl.loop(1, group)
        def _(p):
            pltpu.make_async_remote_copy(
                src_ref=back.at[k, p], dst_ref=ent.at[k, group - p],
                send_sem=b_send.at[k], recv_sem=b_recv.at[k],
                device_id={"seq": base + lax.rem(mine + p, group)},
                device_id_type=pl.DeviceIdType.MESH).start()

    def correct(k):
        drain(ent, k, b_recv)
        ents = [ent[k, lax.rem(n - mine + group, group)] for n in range(states)]

        def body(it, es):
            es = list(es)
            for i in range(UNROLL):
                t = it * UNROLL + i
                acc = [tile(ys, k, t), None]
                for n in range(states):
                    es[n] = fades[k, cell(t, n), :] * es[n]
                    term = cs[n, pl.ds(t, 1), :] * es[n]
                    acc[n % 2] = term if acc[n % 2] is None else acc[n % 2] + term
                ys[k, pl.ds(pl.multiple_of(t * SUB, SUB), SUB), :] = acc[0] + acc[1]
            return tuple(es)

        lax.fori_loop(0, tokens // UNROLL, body, tuple(ents))

    def finish(k):
        @pl.loop(0, lanes_of(k))
        def _(j):
            lo = pl.multiple_of((k * SUB + j) * LANES, LANES)
            cols = pl.ds(lo, LANES)
            y = ys[k, pl.ds(j, tokens, stride=SUB), :]
            g = g_ref[:, cols].astype(F32)
            mixed = (y + skip_ref[:, cols] * u_ref[:, cols].astype(F32)) * (
                g / (1.0 + jnp.exp(-g)))
            out_ref[:, cols] = mixed.astype(out_ref.dtype)

    if inner % TILE:
        sums[blocks - 1] = jnp.zeros((SUB, LANES), F32)
    for k in range(blocks):
        steps(k)
    for n in range(states):
        bs[n] = jnp.broadcast_to(whole[:, rank + n:rank + n + 1], (tokens, LANES))
    for k in range(blocks):
        ends(k)
    for n in range(states):
        cs[n] = jnp.broadcast_to(
            whole[:, rank + states + n:rank + states + n + 1], (tokens, LANES))
    for k in range(blocks):
        local(k)
        if k < blocks - 1 or blocks == 1:
            own(k)
        if k == blocks - 2:
            own(blocks - 1)
    loads[5].wait()
    loads[6].wait()
    for k in range(blocks):
        correct(k)
        finish(k)
    for k in range(blocks):
        drain(got_s, k, s_send)
        drain(got_e, k, e_send)
        drain(back, k, b_send)


def solution(mesh):
    seq, mp = mesh.shape["seq"], mesh.shape["mp"]

    def per_device(inner_act, gate_act, x_proj, dt_proj, dt_bias, a_log, skip):
        tokens, inner = inner_act.shape
        rank, states = dt_proj.shape[0], a_log.shape[0]
        blocks = pl.cdiv(inner, TILE)
        group, groups = states, seq // states
        hbm = pl.BlockSpec(memory_space=pltpu.MemorySpace.HBM)
        args = (inner_act, gate_act, x_proj.T, dt_proj, dt_bias.reshape(1, inner), a_log,
                skip.reshape(1, inner))
        cell = (SUB, LANES)
        dma = pltpu.SemaphoreType.DMA
        return pl.pallas_call(
            functools.partial(kernel, seq, mp, tokens, inner, rank, states),
            out_shape=jax.ShapeDtypeStruct((tokens, inner), jnp.bfloat16),
            in_specs=[hbm] * len(args),
            out_specs=pl.BlockSpec(memory_space=pltpu.VMEM),
            scratch_shapes=[pltpu.VMEM(a.shape, a.dtype) for a in args] + [
                pltpu.VMEM((mp, tokens, x_proj.shape[1]), F32),
                pltpu.VMEM((states, tokens, LANES), F32),
                pltpu.VMEM((states, tokens, LANES), F32),
                pltpu.VMEM((blocks, states * SUB, LANES), F32),
                pltpu.VMEM((tokens, TILE), F32),
                pltpu.VMEM((blocks, tokens * SUB, LANES), F32),
                pltpu.VMEM((blocks, tokens * SUB, LANES), F32),
                pltpu.VMEM((blocks, tokens * SUB, LANES), F32),
                pltpu.VMEM((blocks, tokens * states * SUB, LANES), F32),
                pltpu.VMEM((blocks, states) + cell, F32),
                pltpu.VMEM((blocks,) + cell, F32),
                pltpu.VMEM((blocks, group) + cell, F32),
                pltpu.VMEM((blocks, group) + cell, F32),
                pltpu.VMEM((blocks, group) + cell, F32),
                pltpu.VMEM((blocks, group) + cell, F32),
                pltpu.VMEM((blocks, groups, 2) + cell, F32),
                pltpu.VMEM((blocks, 2) + cell, F32),
                dma((len(args),)),
                dma((mp - 1,)), dma((mp - 1,)),
                dma((blocks,)), dma((blocks,)),
                dma((blocks,)), dma((blocks,)),
                dma((blocks,)), dma((blocks,)),
                dma((blocks, groups)), dma((blocks, groups)),
            ],
            compiler_params=pltpu.CompilerParams(
                collective_id=0, has_side_effects=True,
                vmem_limit_bytes=62 * 1024 * 1024),
        )(*args)

    placed = (
        P("seq", "mp"),
        P("seq", "mp"),
        P("mp", None),
        P(None, "mp"),
        P("mp"),
        P(None, "mp"),
        P("mp"),
    )
    return jax.shard_map(
        per_device, mesh=mesh, in_specs=placed, out_specs=P("seq", "mp"), check_vma=False
    )
```
